128 devices in a mesh: row: 8 (over z_hi, y), col: 16 (over x, z_lo, core).
Axes of the slice: x: 4, y: 4, z: 4 (z_hi: 2, z_lo: 2; z = z_hi * 2 + z_lo), core: 2. Of those that a mesh axis runs over, the one named last changes fastest.
Arguments:
- vectors: bfloat16 [32, 524288], P(None, ('row', 'col')), may hold values from -6 to 6
- tile_values: bfloat16 [81920, 128, 128], P(('row', 'col')), may hold values from -0.0546875 to 0.0546875
- tile_rows: int32 [81920], P(('row', 'col')), may hold values from 0 to 511
- tile_cols: int32 [81920], P(('row', 'col')), may hold values from 0 to 255
- tile_count: int32 [128], P(('row', 'col')), may hold values from 160 to 640, as said below
Outputs:
- filtered: bfloat16 [32, 524288], P(None, ('row', 'col'))
The draws below stay inside these ranges and needn't reach their ends.
Inputs may be any that keep to these rules, and one draw needn't show every extreme that they name: `tile_count`: every device has at least a quarter of its slots live and some device has all 640 live.
All inputs are finite; a program needn't handle non-finite values.
Results may differ from the reference program's by a relative error of at most 0.014.
Values may be sent and summed in bfloat16 or wider, within the bound.
A program may use at most 128 MiB of HBM per device.

```python
import jax
import jax.numpy as jnp
from jax import lax

TILE = 128
K = 32
TPD = 640
NV = 524288
TCH = 32
RP = 512
CP = 256
N_COL = 16
DEVICES = 128


def draw_tile_count(key, part):
    key_counts, key_full = jax.random.split(jax.random.fold_in(key, 7))
    counts = jax.random.randint(key_counts, (DEVICES,), max(1, TPD // 4), TPD + 1)
    full_device = jax.random.randint(key_full, (), 0, DEVICES)
    return jnp.where(jnp.arange(DEVICES) == full_device, TPD, counts).astype(jnp.int32)


def plant(result, stream_key, low, high):
    longest = result.shape.index(max(result.shape))
    spots = []
    for shift in (0, 1):
        where = [jax.random.randint(jax.random.fold_in(stream_key, axis), (), 0, length) for axis, length in enumerate(result.shape)]
        where[longest] = (where[longest] + shift) % result.shape[longest]
        spots.append(tuple(where))
    return result.at[spots[0]].set(low).at[spots[1]].set(high)


def steps_of(rng, dims, cuts, least, top_value):
    factor_of = 1.0
    for dim, blocks in cuts:
        steps = jax.random.uniform(jax.random.fold_in(jax.random.fold_in(rng, 6), dim), (blocks,), jnp.float32, least / len(cuts), top_value / len(cuts))
        factor_of = factor_of * jnp.repeat(jnp.exp(steps), dims[dim] // blocks).reshape((-1,) + (1,) * (len(dims) - 1 - dim))
    return factor_of


def scatter_about(own_key, dims, width, bound, cuts=(), kind=jnp.bfloat16):
    level = steps_of(own_key, dims, cuts, -0.22, 0.18) if cuts else 1.0
    entries = jax.random.normal(own_key, dims, jnp.float32) * width * level
    return jnp.minimum(jnp.maximum(entries, -bound), bound).astype(kind)


def setup_inputs(seed: int = 0) -> dict:
    key_list = jax.random.split(jax.random.key(seed), 6)
    vectors = scatter_about(key_list[0], (K, NV), 1.0, 6.0, ((1, 128),))
    tile_values = scatter_about(key_list[1], (DEVICES * TPD, TILE, TILE), (20 * TPD) ** -0.5, 0.0546875, ((0, 128),))
    tile_rows = plant(jax.random.randint(key_list[2], (DEVICES * TPD,), 0, RP), jax.random.fold_in(key_list[2], 1), 0, RP - 1).astype(jnp.int32)
    tile_cols = plant(jax.random.randint(key_list[3], (DEVICES * TPD,), 0, CP), jax.random.fold_in(key_list[3], 1), 0, CP - 1).astype(jnp.int32)
    tile_count = draw_tile_count(jax.random.fold_in(key_list[5], 71), 0)
    return {"vectors": vectors, "tile_values": tile_values, "tile_rows": tile_rows, "tile_cols": tile_cols, "tile_count": tile_count}


def reference(vectors, tile_values, tile_rows, tile_cols, tile_count):
    all_blocks = NV // TILE
    x_blocks = vectors.astype(jnp.float32).reshape(K, all_blocks, TILE)
    tiles_all = tile_values.reshape(DEVICES, TPD, TILE, TILE)
    rows_all = tile_rows.reshape(DEVICES, TPD)
    cols_all = tile_cols.reshape(DEVICES, TPD)

    def visit(accumulated, device_item):
        device_id, tile_block, row_ids, col_ids, live_count = device_item
        grid_row = device_id // N_COL
        grid_col = device_id % N_COL
        global_rows = (grid_row * RP + row_ids).astype(jnp.int32)
        global_cols = (((col_ids // TCH) * N_COL + grid_col) * TCH + col_ids % TCH).astype(jnp.int32)
        alive = (jnp.arange(TPD, dtype=jnp.int32) < live_count).astype(jnp.float32)
        masked_tiles = tile_block.astype(jnp.float32) * alive[:, None, None]
        x_col = x_blocks[:, global_cols, :]
        x_row = x_blocks[:, global_rows, :]
        to_rows = jnp.einsum('ktj,tij->kti', x_col, masked_tiles, precision=lax.Precision.HIGHEST)
        to_cols = jnp.einsum('kti,tij->ktj', x_row, masked_tiles, precision=lax.Precision.HIGHEST)
        row_part = jnp.zeros((K, RP, TILE), jnp.float32).at[:, row_ids, :].add(to_rows)
        col_part = jnp.zeros((K, CP, TILE), jnp.float32).at[:, col_ids, :].add(to_cols)
        row_part = lax.optimization_barrier(row_part.astype(jnp.bfloat16)).astype(jnp.float32)
        col_part = lax.optimization_barrier(col_part.astype(jnp.bfloat16)).astype(jnp.float32)
        panel_rows = (grid_row * RP + jnp.arange(RP, dtype=jnp.int32)).astype(jnp.int32)
        local_cols = jnp.arange(CP, dtype=jnp.int32)
        panel_cols = (((local_cols // TCH) * N_COL + grid_col) * TCH + local_cols % TCH).astype(jnp.int32)
        accumulated = accumulated.at[:, panel_rows, :].add(row_part)
        accumulated = accumulated.at[:, panel_cols, :].add(col_part)
        return accumulated, None

    start_total = jnp.zeros((K, all_blocks, TILE), jnp.float32)
    device_ids = jnp.arange(DEVICES, dtype=jnp.int32)
    total, _ = lax.scan(visit, start_total, (device_ids, tiles_all, rows_all, cols_all, tile_count))
    return total.reshape(K, NV).astype(jnp.bfloat16)
```

```python
import jax
import jax.numpy as jnp
from jax import lax
from jax.experimental import pallas as pl
from jax.experimental.pallas import tpu as pltpu
from jax.sharding import PartitionSpec as P

MESH = pl.DeviceIdType.MESH
VMEM = pltpu.VMEM
HALF = 16
CHUNK = 32
UNROLL = 16
RING = 8


def place():
    row, col = lax.axis_index("row"), lax.axis_index("col")
    return row % 4, row // 4, col // 4, (col // 2) % 2, col % 2


def col_of(x, zl, core):
    return lax.rem(x, 4) * 4 + zl * 2 + core


def row_of(y, zh):
    return zh * 4 + lax.rem(y, 4)


class Net:
    def __init__(self):
        self.y, self.zh, self.x, self.zl, self.core = y, zh, x, zl, core = place()
        row, col = lax.axis_index("row"), lax.axis_index("col")
        self.row, self.col = row, col
        self.right = (row, col_of(x + 1, zl, core))
        self.left = (row, col_of(x + 3, zl, core))
        self.zpair = (row, col_of(x, 1 - zl, core))
        self.mate = (row, col_of(x, zl, 1 - core))
        self.up = (row_of(y + 1, zh), col)
        self.down = (row_of(y + 3, zh), col)
        self.zfar = (row_of(y, 1 - zh), col)

    def own_col(self, dx, p):
        return col_of(self.x + dx, self.zl if p == 0 else 1 - self.zl, self.core)

    def mate_col(self, dx, p):
        return col_of(self.x + dx, self.zl if p == 0 else 1 - self.zl, 1 - self.core)

    def own_row(self, dy, q):
        return row_of(self.y + dy, self.zh if q == 0 else 1 - self.zh)

    def barrier(self):
        sem = pltpu.get_barrier_semaphore()
        peers = (self.right, self.left, self.zpair, self.mate, self.up, self.down, self.zfar)
        for peer in peers:
            pl.semaphore_signal(sem, inc=1, device_id=peer, device_id_type=MESH)
        pl.semaphore_wait(sem, len(peers))


class Sends:
    def __init__(self, sems):
        self.sems, self.copies = sems, []

    def __call__(self, src, dst, recv, peer):
        copy = pltpu.make_async_remote_copy(
            src_ref=src,
            dst_ref=dst,
            send_sem=self.sems.at[len(self.copies)],
            recv_sem=recv,
            device_id=peer,
            device_id_type=MESH,
        )
        copy.start()
        self.copies.append(copy)

    def drain(self):
        for copy in self.copies:
            copy.wait_send()


def await_copy(ref, sem):
    pltpu.make_async_copy(ref, ref, sem).wait()


def half(h):
    return pl.ds(HALF * h, HALF)


GATHER_SENDS = 44


def gather_kernel(v, xr, xc, keep, send_sems, z_in, x_in, fx_in, m_in, zf_in, y_in, fy_in):
    net = Net()
    send = Sends(send_sems)

    def r_at(dx, p, h):
        return xr.at[net.own_col(dx, p), half(h)]

    def m_at(dx, p, h):
        return xr.at[net.mate_col(dx, p), half(h)]

    def c_at(dy, q, h):
        return xc.at[net.own_row(dy, q), half(h)]

    own = [
        pltpu.make_async_copy(v, xr.at[net.col], keep.at[0]),
        pltpu.make_async_copy(v, xc.at[net.row], keep.at[1]),
    ]
    net.barrier()
    for h in range(2):
        send(v.at[half(h)], c_at(0, 0, h), zf_in.at[h], net.zfar)
    for i in range(2):
        for h, way, x_peer, y_peer in ((i, 0, net.right, net.up), (1 - i, 1, net.left, net.down)):
            send(v.at[half(h)], r_at(0, 0, h), x_in.at[way, 0, h], x_peer)
            send(v.at[half(h)], c_at(0, 0, h), y_in.at[way, 0, h], y_peer)
    for h in range(2):
        send(v.at[half(h)], r_at(0, 0, h), z_in.at[0, h], net.zpair)
    for h in range(2):
        send(v.at[half(h)], r_at(0, 0, h), m_in.at[0, 0, h], net.mate)
    for copy in own:
        copy.start()

    def pass_on(dx, p, h, sem, peer):
        send(r_at(dx, p, h), r_at(dx, p, h), sem, peer)

    def pass_up(dy, q, h, sem, peer):
        send(c_at(dy, q, h), c_at(dy, q, h), sem, peer)

    def to_mate(dx, p, h):
        pass_on(dx, p, h, m_in.at[dx, p, h], net.mate)

    def x_came(way, p, h):
        dx = 3 if way == 0 else 1
        await_copy(r_at(dx, p, h), x_in.at[way, p, h])
        if p == 0 and h == way:
            pass_on(dx, 0, h, fx_in.at[way], net.right if way == 0 else net.left)
        to_mate(dx, p, h)

    def y_came(way, q, h):
        dy = 3 if way == 0 else 1
        await_copy(c_at(dy, q, h), y_in.at[way, q, h])
        if h == way:
            pass_up(dy, q, h, fy_in.at[way, q], net.up if way == 0 else net.down)

    for way in range(2):
        x_came(way, 0, way)
        y_came(way, 0, way)
    for way in range(2):
        x_came(way, 0, 1 - way)
        y_came(way, 0, 1 - way)
    await_copy(c_at(0, 1, 0), zf_in.at[0])
    pass_up(0, 1, 0, y_in.at[0, 1, 0], net.up)
    await_copy(c_at(0, 1, 1), zf_in.at[1])
    pass_up(0, 1, 1, y_in.at[1, 1, 1], net.down)
    pass_up(0, 1, 1, y_in.at[0, 1, 1], net.up)
    pass_up(0, 1, 0, y_in.at[1, 1, 0], net.down)
    for h in range(2):
        await_copy(r_at(0, 1, h), z_in.at[0, h])
        pass_on(0, 1, h, x_in.at[0, 1, h], net.right)
        pass_on(0, 1, h, x_in.at[1, 1, h], net.left)
        to_mate(0, 1, h)
        await_copy(r_at(2, 0, h), fx_in.at[h])
        pass_on(2, 0, h, z_in.at[1, h], net.zpair)
        to_mate(2, 0, h)
    for way in range(2):
        y_came(way, 1, way)
    for h in range(2):
        for way in range(2):
            x_came(way, 1, h)
    for h in range(2):
        await_copy(r_at(2, 1, h), z_in.at[1, h])
        to_mate(2, 1, h)
    for way in range(2):
        await_copy(c_at(2, 0, way), fy_in.at[way, 0])
        y_came(way, 1, 1 - way)
    for h in range(2):
        await_copy(c_at(2, 1, h), fy_in.at[h, 1])
    for dx in (0, 3, 1, 2):
        for p in range(2):
            for h in range(2):
                await_copy(m_at(dx, p, h), m_in.at[dx, p, h])
    for copy in own:
        copy.wait()
    send.drain()
    assert len(send.copies) == GATHER_SENDS


def gather(v):
    k, n = v.shape
    dma = pltpu.SemaphoreType.DMA
    return pl.pallas_call(
        gather_kernel,
        out_shape=[jax.ShapeDtypeStruct((16, k, n), v.dtype), jax.ShapeDtypeStruct((8, k, n), v.dtype)],
        in_specs=[pl.BlockSpec(memory_space=VMEM)],
        out_specs=[pl.BlockSpec(memory_space=pl.ANY)] * 2,
        scratch_shapes=[
            dma((2,)),
            dma((GATHER_SENDS,)),
            dma((2, 2)),
            dma((2, 2, 2)),
            dma((2,)),
            dma((4, 2, 2)),
            dma((2,)),
            dma((2, 2, 2)),
            dma((2, 2)),
        ],
        compiler_params=pltpu.CompilerParams(collective_id=0, has_side_effects=True, vmem_limit_bytes=4 << 20),
        name="panels",
    )(v)


def product_kernel(count, rows, cols, xr, xc, tiles_hbm, out_r, out_c, tiles, acc_r, acc_c, sems):
    live = count[0]
    chunks = (live + CHUNK - 1) // CHUNK

    def fetch(i):
        n = lax.rem(i, RING)
        return pltpu.make_async_copy(tiles_hbm.at[pl.ds(i * CHUNK, CHUNK)], tiles.at[n], sems.at[n])

    @pl.loop(0, jnp.minimum(chunks, RING))
    def _(i):
        fetch(i).start()

    @pl.loop(0, 16)
    def _(i):
        acc_r[i] = jnp.zeros(acc_r.shape[1:], jnp.float32)

    @pl.loop(0, 8)
    def _(i):
        acc_c[i] = jnp.zeros(acc_c.shape[1:], jnp.float32)

    def lanes(block):
        return pl.ds(pl.multiple_of(lax.rem(block, 32) * 128, 128), 128)

    none = jnp.zeros((32, 128), jnp.bfloat16)

    def both(x, y):
        return jnp.concatenate([jnp.concatenate([x, none], axis=1), jnp.concatenate([none, y], axis=1)], axis=0)

    @pl.loop(0, chunks)
    def _(i):
        fetch(i).wait()
        n = lax.rem(i, RING)

        @pl.loop(0, CHUNK // UNROLL)
        def _(j):
            found = []
            for u in range(0, UNROLL, 2):
                at = j * UNROLL + u
                s = i * CHUNK + at
                rb, cb = [rows[s], rows[s + 1]], [cols[s], cols[s + 1]]
                t = tiles[n, pl.ds(at, 2)]
                x_c = both(*[xc[b // 32, :, lanes(b)] for b in cb])
                x_r = both(*[xr[b // 32, :, lanes(b)] for b in rb])
                wide = jnp.concatenate([t[0], t[1]], axis=1)
                to_r = lax.dot_general(x_c, wide, (((1,), (1,)), ((), ())), preferred_element_type=jnp.float32)
                tall = t.reshape(256, 128)
                to_c = lax.dot_general(x_r, tall, (((1,), (0,)), ((), ())), preferred_element_type=jnp.float32)
                for e in range(2):
                    part = slice(32 * e, 32 * e + 32)
                    found.append((rb[e], cb[e], s + e < live, to_r[part], to_c[part]))
            for rb, cb, ok, to_r, to_c in found:
                rd = jnp.where(ok, rb // 32, 16)
                cd = jnp.where(ok, cb // 32, 8)
                acc_r[rd, :, lanes(rb)] += to_r
                acc_c[cd, :, lanes(cb)] += to_c

        @pl.when(i + RING < chunks)
        def _():
            fetch(i + RING).start()

    @pl.loop(0, 16)
    def _(i):
        out_r[i] = acc_r[i].astype(jnp.bfloat16)

    @pl.loop(0, 8)
    def _(i):
        out_c[i] = acc_c[i].astype(jnp.bfloat16)


def products(count, rows, cols, xr, xc, tiles):
    k, n = xr.shape[1:]
    smem = pl.BlockSpec(memory_space=pltpu.SMEM)
    vmem = pl.BlockSpec(memory_space=VMEM)
    return pl.pallas_call(
        product_kernel,
        out_shape=[jax.ShapeDtypeStruct(xr.shape, xr.dtype), jax.ShapeDtypeStruct(xc.shape, xc.dtype)],
        in_specs=[smem, smem, smem, vmem, vmem, pl.BlockSpec(memory_space=pl.ANY)],
        out_specs=[vmem, vmem],
        scratch_shapes=[
            VMEM((RING, CHUNK) + tiles.shape[1:], tiles.dtype),
            VMEM((17, k, n), jnp.float32),
            VMEM((9, k, n), jnp.float32),
            pltpu.SemaphoreType.DMA((RING,)),
        ],
        compiler_params=pltpu.CompilerParams(vmem_limit_bytes=40 << 20),
        name="products",
    )(count, rows, cols, xr, xc, tiles)


REDUCE_SENDS = 44


def add_into(dst, index, *others):
    total = dst[index].astype(jnp.float32)
    for ref, at in others:
        total += ref[at].astype(jnp.float32)
    dst[index] = total.astype(jnp.bfloat16)


def reduce_kernel(
    pr, pc, out, a, b, m_buf, x_half, x_buf, z_buf, y_half, y_buf, zf_buf,
    load, send_sems, m_in, fx_in, x_in, z_in, fy_in, y_in, zf_in,
):
    net = Net()
    send = Sends(send_sems)
    order = ((1, 1), (3, 1), (2, 1), (2, 0), (1, 0), (3, 0), (0, 1), (0, 0))
    loads = {}
    for n, (d, p) in enumerate(order):
        loads[d, p] = [
            pltpu.make_async_copy(pr.at[net.own_col(d, p)], a.at[d, p], load.at[0, n]),
            pltpu.make_async_copy(pc.at[net.own_row(d, p)], b.at[d, p], load.at[1, n]),
        ]
        for copy in loads[d, p]:
            copy.start()
    net.barrier()
    for d, p in order:
        for h in range(2):
            send(pr.at[net.mate_col(d, p), half(h)], m_buf.at[d, p, half(h)], m_in.at[d, p, h], net.mate)

    def from_mate(d, p, h):
        await_copy(m_buf.at[d, p, half(h)], m_in.at[d, p, h])
        add_into(a, (d, p, half(h)), (m_buf, (d, p, half(h))))

    x_peers, y_peers = (net.right, net.left), (net.up, net.down)
    dist = (1, 3)

    def x_send(way, p, h):
        d = dist[way]
        send(a.at[d, p, half(h)], x_buf.at[way, p, half(h)], x_in.at[way, p, h], x_peers[way])

    def y_send(way, q, h):
        d = dist[way]
        send(b.at[d, q, half(h)], y_buf.at[way, q, half(h)], y_in.at[way, q, h], y_peers[way])

    def y_far(way, q):
        send(b.at[2, q, half(way)], y_half.at[way, q], fy_in.at[way, q], y_peers[way])

    def y_join(way, q):
        await_copy(y_half.at[way, q], fy_in.at[way, q])
        add_into(b, (dist[way], q, half(way)), (y_half, (way, q)))
        y_send(way, q, way)

    loads[2, 1][1].wait()
    for way in range(2):
        y_far(way, 1)
    for way in range(2):
        loads[dist[way], 1][1].wait()
        y_send(way, 1, 1 - way)
    for way in range(2):
        loads[dist[way], 1][0].wait()
        for h in range(2):
            from_mate(dist[way], 1, h)
            x_send(way, 1, h)
    loads[2, 1][0].wait()
    for h in range(2):
        from_mate(2, 1, h)
        send(a.at[2, 1, half(h)], z_buf.at[1, half(h)], z_in.at[1, h], net.zpair)
    for way in range(2):
        y_join(way, 1)
    for way in range(2):
        loads[dist[way], 0][0].wait()
        from_mate(dist[way], 0, 1 - way)
        x_send(way, 0, 1 - way)
    loads[2, 0][1].wait()
    for way in range(2):
        y_far(way, 0)
    for way in range(2):
        loads[dist[way], 0][1].wait()
        y_send(way, 0, 1 - way)
    loads[2, 0][0].wait()
    for way in range(2):
        from_mate(2, 0, way)
        await_copy(z_buf.at[1, half(way)], z_in.at[1, way])
        add_into(a, (2, 0, half(way)), (z_buf, (1, half(way))))
        send(a.at[2, 0, half(way)], x_half.at[way], fx_in.at[way], x_peers[way])
    for way in range(2):
        from_mate(dist[way], 0, way)
    for p in (1, 0):
        loads[0, p][0].wait()
        loads[0, p][1].wait()
        for h in range(2):
            from_mate(0, p, h)

    def x_total(p, h):
        for way in range(2):
            await_copy(x_buf.at[way, p, half(h)], x_in.at[way, p, h])
        add_into(a, (0, p, half(h)), (x_buf, (0, p, half(h))), (x_buf, (1, p, half(h))))

    def y_total(q, h):
        for way in range(2):
            await_copy(y_buf.at[way, q, half(h)], y_in.at[way, q, h])
        add_into(b, (0, q, half(h)), (y_buf, (0, q, half(h))), (y_buf, (1, q, half(h))))

    for h in range(2):
        x_total(1, h)
        send(a.at[0, 1, half(h)], z_buf.at[0, half(h)], z_in.at[0, h], net.zpair)
    for h in range(2):
        y_total(1, h)
        send(b.at[0, 1, half(h)], zf_buf.at[half(h)], zf_in.at[h], net.zfar)
    for way in range(2):
        await_copy(x_half.at[way], fx_in.at[way])
        add_into(a, (dist[way], 0, half(way)), (x_half, (way,)))
        x_send(way, 0, way)
        y_join(way, 0)
    for h in range(2):
        x_total(0, h)
        y_total(0, h)
        await_copy(z_buf.at[0, half(h)], z_in.at[0, h])
        await_copy(zf_buf.at[half(h)], zf_in.at[h])
        total = a[0, 0, half(h)].astype(jnp.float32) + z_buf[0, half(h)].astype(jnp.float32)
        total += b[0, 0, half(h)].astype(jnp.float32)
        total += zf_buf[half(h)].astype(jnp.float32)
        out[half(h)] = total.astype(jnp.bfloat16)
    send.drain()
    assert len(send.copies) == REDUCE_SENDS, len(send.copies)


def reduce_scatter(pr, pc):
    k, n = pr.shape[1:]
    dma = pltpu.SemaphoreType.DMA
    blk = lambda *lead: VMEM((*lead, k, n), jnp.bfloat16)
    hlf = lambda *lead: VMEM((*lead, HALF, n), jnp.bfloat16)
    return pl.pallas_call(
        reduce_kernel,
        out_shape=jax.ShapeDtypeStruct((k, n), jnp.bfloat16),
        in_specs=[pl.BlockSpec(memory_space=pl.ANY)] * 2,
        out_specs=pl.BlockSpec(memory_space=VMEM),
        scratch_shapes=[
            blk(4, 2), blk(4, 2), blk(4, 2), hlf(2), blk(2, 2), blk(2), hlf(2, 2), blk(2, 2), blk(),
            dma((2, 8)), dma((REDUCE_SENDS,)), dma((4, 2, 2)), dma((2,)), dma((2, 2, 2)), dma((2, 2)),
            dma((2, 2)), dma((2, 2, 2)), dma((2,)),
        ],
        compiler_params=pltpu.CompilerParams(collective_id=1, has_side_effects=True, vmem_limit_bytes=16 << 20),
        name="panel_sums",
    )(pr, pc)


def shards(vectors, tile_values, tile_rows, tile_cols, tile_count):
    xr, xc = gather(vectors)
    pr, pc = products(tile_count, tile_rows, tile_cols, xr, xc, tile_values)
    return reduce_scatter(pr, pc)


def solution(mesh):
    in_specs = (
        P(None, ("row", "col")),
        P(("row", "col"), None, None),
        P(("row", "col")),
        P(("row", "col")),
        P(("row", "col")),
    )
    out_specs = P(None, ("row", "col"))
    return jax.shard_map(shards, mesh=mesh, in_specs=in_specs, out_specs=out_specs, check_vma=False)
```

```python
import jax
import jax.numpy as jnp
from jax import lax
from jax.experimental import pallas as pl
from jax.experimental.pallas import tpu as pltpu
from jax.sharding import PartitionSpec as P

MESH = pl.DeviceIdType.MESH
VMEM = pltpu.VMEM
HALF = 16
CHUNK = 32
UNROLL = 16
GROUPS = CHUNK // UNROLL


def place():
    row, col = lax.axis_index("row"), lax.axis_index("col")
    return row % 4, row // 4, col // 4, (col // 2) % 2, col % 2


def col_of(x, zl, core):
    return lax.rem(x, 4) * 4 + zl * 2 + core


def row_of(y, zh):
    return zh * 4 + lax.rem(y, 4)


class Net:
    def __init__(self):
        self.y, self.zh, self.x, self.zl, self.core = y, zh, x, zl, core = place()
        row, col = lax.axis_index("row"), lax.axis_index("col")
        self.row, self.col = row, col
        self.right = (row, col_of(x + 1, zl, core))
        self.left = (row, col_of(x + 3, zl, core))
        self.zpair = (row, col_of(x, 1 - zl, core))
        self.mate = (row, col_of(x, zl, 1 - core))
        self.up = (row_of(y + 1, zh), col)
        self.down = (row_of(y + 3, zh), col)
        self.zfar = (row_of(y, 1 - zh), col)

    def own_col(self, dx, p):
        return col_of(self.x + dx, self.zl if p == 0 else 1 - self.zl, self.core)

    def mate_col(self, dx, p):
        return col_of(self.x + dx, self.zl if p == 0 else 1 - self.zl, 1 - self.core)

    def own_row(self, dy, q):
        return row_of(self.y + dy, self.zh if q == 0 else 1 - self.zh)

    def barrier(self):
        sem = pltpu.get_barrier_semaphore()
        peers = (self.right, self.left, self.zpair, self.mate, self.up, self.down, self.zfar)
        for peer in peers:
            pl.semaphore_signal(sem, inc=1, device_id=peer, device_id_type=MESH)
        pl.semaphore_wait(sem, len(peers))


class Sends:
    def __init__(self, sems):
        self.sems, self.copies = sems, []

    def __call__(self, src, dst, recv, peer):
        copy = pltpu.make_async_remote_copy(
            src_ref=src,
            dst_ref=dst,
            send_sem=self.sems.at[len(self.copies)],
            recv_sem=recv,
            device_id=peer,
            device_id_type=MESH,
        )
        copy.start()
        self.copies.append(copy)

    def drain(self):
        for copy in self.copies:
            copy.wait_send()


def await_copy(ref, sem):
    pltpu.make_async_copy(ref, ref, sem).wait()


def half(h):
    return pl.ds(HALF * h, HALF)


GATHER_SENDS = 44
TILE_COPIES = 4
VMEM_GRANT = 18 << 20


def gather_kernel(v, rows_hbm, cols_hbm, tiles_hbm, xr, xc, rows, cols, tiles, keep, send_sems, z_in, x_in, fx_in, m_in, zf_in, y_in, fy_in):
    net = Net()
    send = Sends(send_sems)

    def r_at(dx, p, h):
        return xr.at[net.own_col(dx, p), half(h)]

    def m_at(dx, p, h):
        return xr.at[net.mate_col(dx, p), half(h)]

    def c_at(dy, q, h):
        return xc.at[net.own_row(dy, q), half(h)]

    own = [
        pltpu.make_async_copy(v, xr.at[net.col], keep.at[0]),
        pltpu.make_async_copy(v, xc.at[net.row], keep.at[1]),
        pltpu.make_async_copy(rows_hbm, rows, keep.at[2]),
        pltpu.make_async_copy(cols_hbm, cols, keep.at[3]),
    ]
    for i in range(TILE_COPIES):
        part = pl.ds(i * (tiles.shape[0] // TILE_COPIES), tiles.shape[0] // TILE_COPIES)
        own.append(pltpu.make_async_copy(tiles_hbm.at[part], tiles.at[part], keep.at[4 + i]))
    net.barrier()
    for h in range(2):
        send(v.at[half(h)], c_at(0, 0, h), zf_in.at[h], net.zfar)
    for i in range(2):
        for h, way, x_peer, y_peer in ((i, 0, net.right, net.up), (1 - i, 1, net.left, net.down)):
            send(v.at[half(h)], r_at(0, 0, h), x_in.at[way, 0, h], x_peer)
            send(v.at[half(h)], c_at(0, 0, h), y_in.at[way, 0, h], y_peer)
    for h in range(2):
        send(v.at[half(h)], r_at(0, 0, h), z_in.at[0, h], net.zpair)
    for h in range(2):
        send(v.at[half(h)], r_at(0, 0, h), m_in.at[0, 0, h], net.mate)
    for copy in own:
        copy.start()

    def pass_on(dx, p, h, sem, peer):
        send(r_at(dx, p, h), r_at(dx, p, h), sem, peer)

    def pass_up(dy, q, h, sem, peer):
        send(c_at(dy, q, h), c_at(dy, q, h), sem, peer)

    def to_mate(dx, p, h):
        pass_on(dx, p, h, m_in.at[dx, p, h], net.mate)

    def x_came(way, p, h):
        dx = 3 if way == 0 else 1
        await_copy(r_at(dx, p, h), x_in.at[way, p, h])
        if p == 0 and h == way:
            pass_on(dx, 0, h, fx_in.at[way], net.right if way == 0 else net.left)
        to_mate(dx, p, h)

    def y_came(way, q, h):
        dy = 3 if way == 0 else 1
        await_copy(c_at(dy, q, h), y_in.at[way, q, h])
        if h == way:
            pass_up(dy, q, h, fy_in.at[way, q], net.up if way == 0 else net.down)

    for way in range(2):
        x_came(way, 0, way)
        y_came(way, 0, way)
    for way in range(2):
        x_came(way, 0, 1 - way)
        y_came(way, 0, 1 - way)
    await_copy(c_at(0, 1, 0), zf_in.at[0])
    pass_up(0, 1, 0, y_in.at[0, 1, 0], net.up)
    await_copy(c_at(0, 1, 1), zf_in.at[1])
    pass_up(0, 1, 1, y_in.at[1, 1, 1], net.down)
    pass_up(0, 1, 1, y_in.at[0, 1, 1], net.up)
    pass_up(0, 1, 0, y_in.at[1, 1, 0], net.down)
    for h in range(2):
        await_copy(r_at(0, 1, h), z_in.at[0, h])
        pass_on(0, 1, h, x_in.at[0, 1, h], net.right)
        pass_on(0, 1, h, x_in.at[1, 1, h], net.left)
        to_mate(0, 1, h)
        await_copy(r_at(2, 0, h), fx_in.at[h])
        pass_on(2, 0, h, z_in.at[1, h], net.zpair)
        to_mate(2, 0, h)
    for way in range(2):
        y_came(way, 1, way)
    for h in range(2):
        for way in range(2):
            x_came(way, 1, h)
    for h in range(2):
        await_copy(r_at(2, 1, h), z_in.at[1, h])
        to_mate(2, 1, h)
    for way in range(2):
        await_copy(c_at(2, 0, way), fy_in.at[way, 0])
        y_came(way, 1, 1 - way)
    for h in range(2):
        await_copy(c_at(2, 1, h), fy_in.at[h, 1])
    for dx in (0, 3, 1, 2):
        for p in range(2):
            for h in range(2):
                await_copy(m_at(dx, p, h), m_in.at[dx, p, h])
    for copy in own:
        copy.wait()
    send.drain()
    assert len(send.copies) == GATHER_SENDS


def gather(v, rows, cols, tiles):
    k, n = v.shape
    dma = pltpu.SemaphoreType.DMA
    return pl.pallas_call(
        gather_kernel,
        out_shape=[jax.ShapeDtypeStruct((16, k, n), v.dtype), jax.ShapeDtypeStruct((8, k, n), v.dtype)]
        + [jax.ShapeDtypeStruct(a.shape, a.dtype) for a in (rows, cols, tiles)],
        in_specs=[pl.BlockSpec(memory_space=pltpu.HBM)] * 4,
        out_specs=[pl.BlockSpec(memory_space=pl.ANY)] * 5,
        scratch_shapes=[
            dma((4 + TILE_COPIES,)),
            dma((GATHER_SENDS,)),
            dma((2, 2)),
            dma((2, 2, 2)),
            dma((2,)),
            dma((4, 2, 2)),
            dma((2,)),
            dma((2, 2, 2)),
            dma((2, 2)),
        ],
        compiler_params=pltpu.CompilerParams(collective_id=0, has_side_effects=True, vmem_limit_bytes=VMEM_GRANT),
        name="panels",
    )(v, rows, cols, tiles)


def product_kernel(count, rows_hbm, cols_hbm, xr, xc, tiles, out_r, out_c, rows, cols, acc_r, acc_c,
                   stage_r0, stage_c0, stage_r1, stage_c1, sems):
    lists = [
        pltpu.make_async_copy(rows_hbm, rows, sems.at[0]),
        pltpu.make_async_copy(cols_hbm, cols, sems.at[1]),
    ]
    for copy in lists:
        copy.start()
    live = count[0]
    chunks = (live + CHUNK - 1) // CHUNK

    @pl.loop(0, 16)
    def _(i):
        acc_r[i] = jnp.zeros(acc_r.shape[1:], jnp.float32)

    @pl.loop(0, 8)
    def _(i):
        acc_c[i] = jnp.zeros(acc_c.shape[1:], jnp.float32)

    for copy in lists:
        copy.wait()

    def lanes(block):
        return pl.ds(pl.multiple_of((block & 31) * 128, 128), 128)

    none = jnp.zeros((32, 128), jnp.bfloat16)

    def both(x, y):
        return jnp.concatenate([jnp.concatenate([x, none], axis=1), jnp.concatenate([none, y], axis=1)], axis=0)

    def multiply(s, u, stage_r, stage_c):
        rb, cb = [rows[s], rows[s + 1]], [cols[s], cols[s + 1]]
        t = tiles[pl.ds(s, 2)]
        x_c = both(*[xc[b >> 5, :, lanes(b)] for b in cb])
        x_r = both(*[xr[b >> 5, :, lanes(b)] for b in rb])
        flip = jnp.concatenate([t[0].T, t[1].T], axis=0)
        to_r = lax.dot_general(x_c, flip, (((1,), (0,)), ((), ())), preferred_element_type=jnp.float32)
        tall = t.reshape(256, 128)
        to_c = lax.dot_general(x_r, tall, (((1,), (0,)), ((), ())), preferred_element_type=jnp.float32)
        stage_r[pl.ds(32 * u, 64)] = to_r
        stage_c[pl.ds(32 * u, 64)] = to_c

    def add_up(g, u, stage_r, stage_c):
        s = jnp.maximum(g, 0) * UNROLL + u
        ok = (g >= 0) & (s < live)
        rb, cb = rows[s], cols[s]
        rd = jnp.where(ok, rb >> 5, 16)
        cd = jnp.where(ok, cb >> 5, 8)
        acc_r[rd, :, lanes(rb)] += stage_r[pl.ds(32 * u, 32)]
        acc_c[cd, :, lanes(cb)] += stage_c[pl.ds(32 * u, 32)]

    stages = ((stage_r0, stage_c0), (stage_r1, stage_c1))

    @pl.loop(0, chunks)
    def _(i):
        for part in range(GROUPS):
            for u in range(0, UNROLL, 2):
                multiply(i * CHUNK + part * UNROLL + u, u, *stages[part % 2])
                for e in range(2):
                    add_up(i * GROUPS + part - 1, u + e, *stages[1 - part % 2])

    for u in range(UNROLL):
        add_up(chunks * GROUPS - 1, u, *stages[(GROUPS - 1) % 2])

    @pl.loop(0, 16)
    def _(i):
        out_r[i] = acc_r[i].astype(jnp.bfloat16)

    @pl.loop(0, 8)
    def _(i):
        out_c[i] = acc_c[i].astype(jnp.bfloat16)


def products(count, rows, cols, xr, xc, tiles):
    k, n = xr.shape[1:]
    smem = pl.BlockSpec(memory_space=pltpu.SMEM)
    vmem = pl.BlockSpec(memory_space=VMEM)
    keep = pl.BlockSpec(memory_space=pl.ANY)
    return pl.pallas_call(
        product_kernel,
        out_shape=[jax.ShapeDtypeStruct(xr.shape, xr.dtype), jax.ShapeDtypeStruct(xc.shape, xc.dtype)],
        in_specs=[smem, keep, keep, vmem, vmem, vmem],
        out_specs=[vmem, vmem],
        scratch_shapes=[
            pltpu.SMEM(rows.shape, rows.dtype),
            pltpu.SMEM(cols.shape, cols.dtype),
            VMEM((17, k, n), jnp.float32),
            VMEM((9, k, n), jnp.float32),
            *[VMEM((32 * UNROLL, 128), jnp.float32)] * 4,
            pltpu.SemaphoreType.DMA((2,)),
        ],
        compiler_params=pltpu.CompilerParams(vmem_limit_bytes=VMEM_GRANT),
        name="products",
    )(count, rows, cols, xr, xc, tiles)


REDUCE_SENDS = 44


def add_into(dst, index, *others):
    total = dst[index].astype(jnp.float32)
    for ref, at in others:
        total += ref[at].astype(jnp.float32)
    dst[index] = total.astype(jnp.bfloat16)


def reduce_kernel(
    pr, pc, out, a, b, m_buf, x_half, x_buf, z_buf, y_half, y_buf, zf_buf,
    load, send_sems, m_in, fx_in, x_in, z_in, fy_in, y_in, zf_in,
):
    net = Net()
    send = Sends(send_sems)
    order = ((1, 1), (3, 1), (2, 1), (2, 0), (1, 0), (3, 0), (0, 1), (0, 0))
    loads = {}
    for n, (d, p) in enumerate(order):
        loads[d, p] = [
            pltpu.make_async_copy(pr.at[net.own_col(d, p)], a.at[d, p], load.at[0, n]),
            pltpu.make_async_copy(pc.at[net.own_row(d, p)], b.at[d, p], load.at[1, n]),
        ]
        for copy in loads[d, p]:
            copy.start()
    net.barrier()
    for d, p in order:
        for h in range(2):
            send(pr.at[net.mate_col(d, p), half(h)], m_buf.at[d, p, half(h)], m_in.at[d, p, h], net.mate)

    def from_mate(d, p, h):
        await_copy(m_buf.at[d, p, half(h)], m_in.at[d, p, h])
        add_into(a, (d, p, half(h)), (m_buf, (d, p, half(h))))

    x_peers, y_peers = (net.right, net.left), (net.up, net.down)
    dist = (1, 3)

    def x_send(way, p, h):
        d = dist[way]
        send(a.at[d, p, half(h)], x_buf.at[way, p, half(h)], x_in.at[way, p, h], x_peers[way])

    def y_send(way, q, h):
        d = dist[way]
        send(b.at[d, q, half(h)], y_buf.at[way, q, half(h)], y_in.at[way, q, h], y_peers[way])

    def y_far(way, q):
        send(b.at[2, q, half(way)], y_half.at[way, q], fy_in.at[way, q], y_peers[way])

    def y_join(way, q):
        await_copy(y_half.at[way, q], fy_in.at[way, q])
        add_into(b, (dist[way], q, half(way)), (y_half, (way, q)))
        y_send(way, q, way)

    loads[2, 1][1].wait()
    for way in range(2):
        y_far(way, 1)
    for way in range(2):
        loads[dist[way], 1][1].wait()
        y_send(way, 1, 1 - way)
    for way in range(2):
        loads[dist[way], 1][0].wait()
        for h in range(2):
            from_mate(dist[way], 1, h)
            x_send(way, 1, h)
    loads[2, 1][0].wait()
    for h in range(2):
        from_mate(2, 1, h)
        send(a.at[2, 1, half(h)], z_buf.at[1, half(h)], z_in.at[1, h], net.zpair)
    for way in range(2):
        y_join(way, 1)
    for way in range(2):
        loads[dist[way], 0][0].wait()
        from_mate(dist[way], 0, 1 - way)
        x_send(way, 0, 1 - way)
    loads[2, 0][1].wait()
    for way in range(2):
        y_far(way, 0)
    for way in range(2):
        loads[dist[way], 0][1].wait()
        y_send(way, 0, 1 - way)
    loads[2, 0][0].wait()
    for way in range(2):
        from_mate(2, 0, way)
        await_copy(z_buf.at[1, half(way)], z_in.at[1, way])
        add_into(a, (2, 0, half(way)), (z_buf, (1, half(way))))
        send(a.at[2, 0, half(way)], x_half.at[way], fx_in.at[way], x_peers[way])
    for way in range(2):
        from_mate(dist[way], 0, way)
    for p in (1, 0):
        loads[0, p][0].wait()
        loads[0, p][1].wait()
        for h in range(2):
            from_mate(0, p, h)

    def x_total(p, h):
        for way in range(2):
            await_copy(x_buf.at[way, p, half(h)], x_in.at[way, p, h])
        add_into(a, (0, p, half(h)), (x_buf, (0, p, half(h))), (x_buf, (1, p, half(h))))

    def y_total(q, h):
        for way in range(2):
            await_copy(y_buf.at[way, q, half(h)], y_in.at[way, q, h])
        add_into(b, (0, q, half(h)), (y_buf, (0, q, half(h))), (y_buf, (1, q, half(h))))

    for h in range(2):
        x_total(1, h)
        send(a.at[0, 1, half(h)], z_buf.at[0, half(h)], z_in.at[0, h], net.zpair)
    for h in range(2):
        y_total(1, h)
        send(b.at[0, 1, half(h)], zf_buf.at[half(h)], zf_in.at[h], net.zfar)
    for way in range(2):
        await_copy(x_half.at[way], fx_in.at[way])
        add_into(a, (dist[way], 0, half(way)), (x_half, (way,)))
        x_send(way, 0, way)
        y_join(way, 0)
    for h in range(2):
        x_total(0, h)
        y_total(0, h)
        await_copy(z_buf.at[0, half(h)], z_in.at[0, h])
        await_copy(zf_buf.at[half(h)], zf_in.at[h])
        total = a[0, 0, half(h)].astype(jnp.float32) + z_buf[0, half(h)].astype(jnp.float32)
        total += b[0, 0, half(h)].astype(jnp.float32)
        total += zf_buf[half(h)].astype(jnp.float32)
        out[half(h)] = total.astype(jnp.bfloat16)
    send.drain()
    assert len(send.copies) == REDUCE_SENDS, len(send.copies)


def reduce_scatter(pr, pc):
    k, n = pr.shape[1:]
    dma = pltpu.SemaphoreType.DMA
    blk = lambda *lead: VMEM((*lead, k, n), jnp.bfloat16)
    hlf = lambda *lead: VMEM((*lead, HALF, n), jnp.bfloat16)
    return pl.pallas_call(
        reduce_kernel,
        out_shape=jax.ShapeDtypeStruct((k, n), jnp.bfloat16),
        in_specs=[pl.BlockSpec(memory_space=pl.ANY)] * 2,
        out_specs=pl.BlockSpec(memory_space=VMEM),
        scratch_shapes=[
            blk(4, 2), blk(4, 2), blk(4, 2), hlf(2), blk(2, 2), blk(2), hlf(2, 2), blk(2, 2), blk(),
            dma((2, 8)), dma((REDUCE_SENDS,)), dma((4, 2, 2)), dma((2,)), dma((2, 2, 2)), dma((2, 2)),
            dma((2, 2)), dma((2, 2, 2)), dma((2,)),
        ],
        compiler_params=pltpu.CompilerParams(collective_id=1, has_side_effects=True, vmem_limit_bytes=16 << 20),
        name="panel_sums",
    )(pr, pc)


def shards(vectors, tile_values, tile_rows, tile_cols, tile_count):
    held = [pltpu.with_memory_space_constraint(a, pltpu.HBM) for a in (vectors, tile_rows, tile_cols, tile_values)]
    xr, xc, rows, cols, tiles = gather(*held)
    pr, pc = products(tile_count, rows, cols, xr, xc, tiles)
    return reduce_scatter(pr, pc)


def solution(mesh):
    in_specs = (
        P(None, ("row", "col")),
        P(("row", "col"), None, None),
        P(("row", "col")),
        P(("row", "col")),
        P(("row", "col")),
    )
    out_specs = P(None, ("row", "col"))
    return jax.shard_map(shards, mesh=mesh, in_specs=in_specs, out_specs=out_specs, check_vma=False)
```
